32 devices in a mesh: groups: 2 (over y), pair: 16 (over z, x, core).
Axes of the slice: x: 2, y: 2, z: 4, core: 2. Of those that a mesh axis runs over, the one named last changes fastest.
Arguments:
- layer_inputs: bfloat16 [64, 4, 2304], P(('groups', 'pair')), parts along dimension 0, may hold values from -6 to 6
- encoder: bfloat16 [4, 2304, 16384], P(None, None, 'pair'), may hold values from -0.125 to 0.125
- enc_bias: float32 [4, 16384], P(None, 'pair'), may hold values from -3 to 3
- decoder: bfloat16 [10, 16384, 2304], P(None, 'pair'), may hold values from -0.03125 to 0.03125
- dec_bias: float32 [4, 2304], replicated, may hold values from -3 to 3
- valid_count: int32 [2], P('groups'), parts along dimension 0, may hold values from 16 to 32
Outputs:
- recon: float32 [64, 4, 2304], P(('groups', 'pair')), parts along dimension 0
The draws below stay inside these ranges and needn't reach their ends.
There are 2 independent parts, one for each index of `groups`. The reference program is written for one: setup_inputs(seed, part) draws one part's arguments, and reference() takes and returns one part's arrays. A program takes and returns all parts, laid end to end along the dimension named above; an argument that names none is the same for every part. Nothing has to cross between parts.
Inputs may be any that keep to these rules, and one draw needn't show every extreme that they name: Tokens at rows valid_count[0] and later are padding.
All inputs are finite; a program needn't handle non-finite values.
Results may differ from the reference program's by a relative error of at most 0.0025.
Values may be sent and summed in bfloat16 or wider, within the bound.
No kernel may reach another device: no remote copies, remote signals or barrier semaphores. Data moves between devices by JAX's collectives and lax.ppermute only.
A program may use at most 192 MiB of HBM per device.

```python
import jax
import jax.numpy as jnp

D = 2304
F = 16384
LAYERS = 4
PAIRS = 10
TOKENS = 32


def block_levels(key, shape, cuts, low, largest):
    factor_of = 1.0
    for dim, blocks in cuts:
        draws = jax.random.uniform(jax.random.fold_in(jax.random.fold_in(key, 6), dim), (blocks,), jnp.float32, low / len(cuts), largest / len(cuts))
        factor_of = factor_of * jnp.repeat(jnp.exp(draws), shape[dim] // blocks).reshape((-1,) + (1,) * (len(shape) - 1 - dim))
    return factor_of


def bell_draw(rng, extent, width, bound, split=(), dtype=jnp.bfloat16):
    loudness = block_levels(rng, extent, split, -0.22, 0.18) if split else 1.0
    result = jax.random.normal(rng, extent, jnp.float32) * width * loudness
    return jnp.minimum(jnp.maximum(result, -bound), bound).astype(dtype)


def setup_inputs(seed: int = 0, part: int = 0) -> dict:
    key_of = jax.random.split(jax.random.key(seed), 7)
    own_keys = jax.random.split(jax.random.fold_in(key_of[6], part), 7)
    layer_inputs = bell_draw(own_keys[0], (TOKENS, LAYERS, D), 1.0, 6.0, ((0, 16),))
    encoder = bell_draw(key_of[1], (LAYERS, D, F), D ** -0.5, 0.125, ((2, 16),))
    enc_bias = bell_draw(key_of[2], (LAYERS, F), 0.5, 3.0, ((1, 16),), jnp.float32)
    decoder = bell_draw(key_of[3], (PAIRS, F, D), (2 * F) ** -0.5, 0.03125, ((1, 16),))
    dec_bias = bell_draw(key_of[4], (LAYERS, D), 0.5, 3.0, (), jnp.float32)
    valid_count = jax.random.randint(own_keys[5], (1,), TOKENS // 2, TOKENS + 1).astype(jnp.int32)
    return dict(layer_inputs=layer_inputs, encoder=encoder, enc_bias=enc_bias, decoder=decoder, dec_bias=dec_bias, valid_count=valid_count)


def pair_index(source, target):
    return source * LAYERS - source * (source - 1) // 2 + (target - source)


def reference(layer_inputs, encoder, enc_bias, decoder, dec_bias, valid_count):
    keep = (jnp.arange(TOKENS).astype(jnp.int32) < valid_count[0])[:, None]
    feats = []
    for source in range(LAYERS):
        pre = jnp.dot(layer_inputs[:, source, :], encoder[source], preferred_element_type=jnp.float32)
        pre = pre + enc_bias[source][None, :]
        feats.append(jnp.where(keep, jnp.maximum(pre, 0.0), 0.0).astype(jnp.bfloat16))
    outputs = []
    for target in range(LAYERS):
        total = jnp.zeros((TOKENS, D), jnp.float32)
        for source in range(target + 1):
            total = total + jnp.dot(feats[source], decoder[pair_index(source, target)], preferred_element_type=jnp.float32)
        outputs.append(total + dec_bias[target][None, :])
    return jnp.stack(outputs, axis=1)
```

```python
import functools

import jax
import jax.numpy as jnp
from jax import lax
from jax.experimental import pallas as pl
from jax.experimental.pallas import tpu as pltpu
from jax.sharding import PartitionSpec as P

BF16, F32 = jnp.bfloat16, jnp.float32
RING = 3


def pair_index(source, target, layers):
    return source * layers - source * (source - 1) // 2 + (target - source)


def swap(value, mask, size):
    return lax.ppermute(value, "pair", [(i, i ^ mask) for i in range(size)])


def kernel(bits, limit, near, far, encoder, bias, decoder, keep_out, send_out, ring, feats, sems):
    layers, half, _ = near.shape
    rows = 2 * half
    block = rows >> bits
    pairs = [(s, t) for t in range(layers) for s in range(t + 1)]

    def fetch(step):
        source, target = pairs[step]
        return pltpu.make_async_copy(
            decoder.at[pair_index(source, target, layers)], ring.at[step % RING], sems.at[step % RING]
        )

    for step in range(min(RING, len(pairs))):
        fetch(step).start()

    row = lax.broadcasted_iota(jnp.int32, (rows, 1), 0)
    slot = row // block
    owner = jnp.zeros_like(slot)
    for bit in range(bits):
        owner = owner | (((slot >> bit) & 1) << (bits - 1 - bit))
    owner = owner ^ lax.axis_index("pair")
    keep = owner * block + row % block < limit[0]

    for layer in range(layers):
        x = jnp.concatenate([near[layer], far[layer]], axis=0)
        pre = jnp.dot(x, encoder[layer], preferred_element_type=F32) + bias[layer][None, :]
        feats[layer] = jnp.where(keep, jnp.maximum(pre, 0.0), 0.0).astype(BF16)

    total = None
    for step, (source, target) in enumerate(pairs):
        fetch(step).wait()
        part = jnp.dot(feats[source], ring[step % RING], preferred_element_type=F32)
        total = part if source == 0 else total + part
        if step + RING < len(pairs):
            fetch(step + RING).start()
        if source == target:
            keep_out[target] = total[:half]
            send_out[target] = total[half:]


def transcode(bits, limit, near, far, encoder, bias, decoder):
    layers, half, width = near.shape
    features = encoder.shape[2]
    vmem = pl.BlockSpec(memory_space=pltpu.VMEM)
    out = jax.ShapeDtypeStruct((layers, half, width), F32)
    need = RING * features * width * 2 + layers * 2 * half * features * 2
    return pl.pallas_call(
        functools.partial(kernel, bits),
        out_shape=(out, out),
        in_specs=[pl.BlockSpec(memory_space=pltpu.SMEM), vmem, vmem, vmem, vmem, pl.BlockSpec(memory_space=pl.ANY)],
        out_specs=(vmem, vmem),
        scratch_shapes=[
            pltpu.VMEM((RING, features, width), BF16),
            pltpu.VMEM((layers, 2 * half, features), BF16),
            pltpu.SemaphoreType.DMA((RING,)),
        ],
        compiler_params=pltpu.CompilerParams(vmem_limit_bytes=need + (6 << 20)),
        name="transcode",
    )(limit, near, far, pltpu.with_memory_space_constraint(encoder, pltpu.VMEM), bias, decoder)


def body(size, layer_inputs, encoder, enc_bias, decoder, dec_bias, valid_count):
    bits = size.bit_length() - 1
    held = jnp.swapaxes(layer_inputs, 0, 1)
    for bit in reversed(range(1, bits)):
        held = jnp.concatenate([held, swap(held, 1 << bit, size)], axis=1)
    far = swap(held, 1, size)
    total, sent = transcode(bits, valid_count, held, far, encoder, enc_bias, decoder)
    for bit in range(bits):
        wide = bit == 0 or bit == bits - 1
        came = swap(sent if wide else sent.astype(BF16), 1 << bit, size)
        total = total + came.astype(F32)
        count = total.shape[1] // 2
        if bit < bits - 1:
            total, sent = total[:, :count], total[:, count:]
    return jnp.swapaxes(total, 0, 1) + dec_bias[None, :, :]


def solution(mesh):
    return jax.shard_map(
        functools.partial(body, mesh.shape["pair"]),
        mesh=mesh,
        in_specs=(
            P(("groups", "pair"), None, None),
            P(None, None, "pair"),
            P(None, "pair"),
            P(None, "pair", None),
            P(),
            P("groups"),
        ),
        out_specs=P(("groups", "pair"), None, None),
        check_vma=False,
    )
```

```python
import functools

import jax
import jax.numpy as jnp
from jax import lax
from jax.experimental import pallas as pl
from jax.experimental.pallas import tpu as pltpu
from jax.sharding import PartitionSpec as P

BF16, F32 = jnp.bfloat16, jnp.float32
RING = 3


def pair_index(source, target, layers):
    return source * layers - source * (source - 1) // 2 + (target - source)


def swap(value, mask, size):
    return lax.ppermute(value, "pair", [(i, i ^ mask) for i in range(size)])


def fetch_kernel(spans, after, source, *rest):
    outs, sems = rest[:-1], rest[-1]
    copies = [
        pltpu.make_async_copy(source.at[pl.ds(start, count)], out, sems.at[i])
        for i, ((start, count), out) in enumerate(zip(spans, outs))
    ]
    for copy in copies:
        copy.start()
    for copy in copies:
        copy.wait()


def fetch_rows(spans, after, source):
    any_space = pl.BlockSpec(memory_space=pl.ANY)
    width = source.shape[1]
    total = sum(count for _, count in spans) * width * 2
    return pl.pallas_call(
        functools.partial(fetch_kernel, spans),
        out_shape=tuple(jax.ShapeDtypeStruct((count, width), source.dtype) for _, count in spans),
        in_specs=[any_space, any_space],
        out_specs=tuple(pl.BlockSpec(memory_space=pltpu.VMEM) for _ in spans),
        scratch_shapes=[pltpu.SemaphoreType.DMA((len(spans),))],
        compiler_params=pltpu.CompilerParams(vmem_limit_bytes=1 << 20),
        cost_estimate=pl.CostEstimate(flops=0, bytes_accessed=2 * total, transcendentals=0),
        name="fetch_rows",
    )(after, pltpu.with_memory_space_constraint(source, pltpu.HBM))


def kernel(bits, pieces, limit, near, far, bias, decoder, *rest):
    encoder = rest[: len(pieces)]
    keep_out, send_out, ring, feats, sems = rest[len(pieces) :]
    layers, half, width = near.shape
    rows = 2 * half
    block = rows >> bits
    pairs = [(s, t) for t in range(layers) for s in range(t + 1)]

    def fetch(step):
        source, target = pairs[step]
        return pltpu.make_async_copy(
            decoder.at[pair_index(source, target, layers)], ring.at[step % RING], sems.at[step % RING]
        )

    for step in range(min(RING, len(pairs))):
        fetch(step).start()

    row = lax.broadcasted_iota(jnp.int32, (rows, 1), 0)
    slot = row // block
    owner = jnp.zeros_like(slot)
    for bit in range(bits):
        owner = owner | (((slot >> bit) & 1) << (bits - 1 - bit))
    owner = owner ^ lax.axis_index("pair")
    keep = owner * block + row % block < limit[0]

    for layer in range(layers):
        x = jnp.concatenate([near[layer], far[layer]], axis=0)
        pre = bias[layer][None, :]
        for (start, count), piece in zip(pieces, encoder):
            first, last = max(start, layer * width), min(start + count, (layer + 1) * width)
            if first < last:
                columns = x[:, first - layer * width : last - layer * width]
                pre = pre + jnp.dot(columns, piece[first - start : last - start], preferred_element_type=F32)
        feats[layer] = jnp.where(keep, jnp.maximum(pre, 0.0), 0.0).astype(BF16)

    total = None
    for step, (source, target) in enumerate(pairs):
        fetch(step).wait()
        part = jnp.dot(feats[source], ring[step % RING], preferred_element_type=F32)
        total = part if source == 0 else total + part
        if step + RING < len(pairs):
            fetch(step + RING).start()
        if source == target:
            keep_out[target] = total[:half]
            send_out[target] = total[half:]


def transcode(bits, pieces, limit, near, far, encoder, bias, decoder):
    layers, half, width = near.shape
    features = decoder.shape[1]
    vmem = pl.BlockSpec(memory_space=pltpu.VMEM)
    out = jax.ShapeDtypeStruct((layers, half, width), F32)
    need = RING * features * width * 2 + layers * 2 * half * features * 2
    return pl.pallas_call(
        functools.partial(kernel, bits, pieces),
        out_shape=(out, out),
        in_specs=[pl.BlockSpec(memory_space=pltpu.SMEM), vmem, vmem, vmem, pl.BlockSpec(memory_space=pl.ANY)]
        + [vmem] * len(pieces),
        out_specs=(vmem, vmem),
        scratch_shapes=[
            pltpu.VMEM((RING, features, width), BF16),
            pltpu.VMEM((layers, 2 * half, features), BF16),
            pltpu.SemaphoreType.DMA((RING,)),
        ],
        compiler_params=pltpu.CompilerParams(vmem_limit_bytes=need + (6 << 20)),
        name="transcode",
    )(limit, near, far, bias, pltpu.with_memory_space_constraint(decoder, pltpu.HBM), *encoder)


def body(size, layer_inputs, encoder, enc_bias, decoder, dec_bias, valid_count):
    bits = size.bit_length() - 1
    held = jnp.swapaxes(layer_inputs, 0, 1)
    layers, width = encoder.shape[:2]
    encoder = encoder.reshape(layers * width, encoder.shape[2])
    steps = list(reversed(range(1, bits)))
    cuts = [2 * layers * i // len(steps) * (width // 2) for i in range(len(steps) + 1)]
    pieces, parts = [], []
    for i, bit in enumerate(steps):
        came = swap(held, 1 << bit, size)
        pieces.append((cuts[i], cuts[i + 1] - cuts[i]))
        (part,) = fetch_rows(pieces[-1:], held, encoder)
        came, part = lax.optimization_barrier((came, part))
        parts.append(part)
        held = jnp.concatenate([held, came], axis=1)
    far = swap(held, 1, size)
    total, sent = transcode(bits, pieces, valid_count, held, far, parts, enc_bias, decoder)
    for bit in range(bits):
        wide = bit == 0 or bit == bits - 1
        came = swap(sent if wide else sent.astype(BF16), 1 << bit, size)
        total = total + came.astype(F32)
        count = total.shape[1] // 2
        if bit < bits - 1:
            total, sent = total[:, :count], total[:, count:]
    return jnp.swapaxes(total, 0, 1) + dec_bias[None, :, :]


def solution(mesh):
    return jax.shard_map(
        functools.partial(body, mesh.shape["pair"]),
        mesh=mesh,
        in_specs=(
            P(("groups", "pair"), None, None),
            P(None, None, "pair"),
            P(None, "pair"),
            P(None, "pair", None),
            P(),
            P("groups"),
        ),
        out_specs=P(("groups", "pair"), None, None),
        check_vma=False,
    )
```

```python
import functools

import jax
import jax.numpy as jnp
from jax import lax
from jax.experimental import pallas as pl
from jax.experimental.pallas import tpu as pltpu
from jax.sharding import PartitionSpec as P

BF16, F32 = jnp.bfloat16, jnp.float32
VMEM = pl.BlockSpec(memory_space=pltpu.VMEM)
SMEM = pl.BlockSpec(memory_space=pltpu.SMEM)
ANY = pl.BlockSpec(memory_space=pl.ANY)
SLOTS = 4


def pair_index(source, target, layers):
    return source * layers - source * (source - 1) // 2 + (target - source)


def in_hbm(value):
    return pltpu.with_memory_space_constraint(value, pltpu.HBM)


def exchange_steps(size):
    masks = [1 << bit for bit in reversed(range(1, size.bit_length() - 1))]
    steps = [(mask, mask) for mask in masks]
    if len(steps) >= 2:
        steps[-2:] = [(masks[-2], masks[-1]), (masks[-1], masks[-2])]
    return steps


def swap(value, masks, size):
    return lax.ppermute(value, "pair", [(i, i ^ masks[i % 2]) for i in range(size)])


def fetch_kernel(indices, *refs):
    count = len(indices)
    sources, outs, sems = refs[1 : 1 + count], refs[1 + count : -1], refs[-1]
    copies = [
        pltpu.make_async_copy(source if index is None else source.at[index], out, sems.at[i])
        for i, (index, source, out) in enumerate(zip(indices, sources, outs))
    ]
    for copy in copies:
        copy.start()
    for copy in copies:
        copy.wait()


def fetch(after, parts, hidden):
    shapes = [jax.ShapeDtypeStruct(a.shape if i is None else a.shape[1:], a.dtype) for a, i in parts]
    return pl.pallas_call(
        functools.partial(fetch_kernel, [index for _, index in parts]),
        out_shape=tuple(shapes),
        in_specs=[ANY] * (1 + len(parts)),
        out_specs=tuple(VMEM for _ in shapes),
        scratch_shapes=[pltpu.SemaphoreType.DMA((len(parts),))],
        compiler_params=pltpu.CompilerParams(vmem_limit_bytes=1 << 20),
        cost_estimate=pl.CostEstimate(flops=0, bytes_accessed=hidden, transcendentals=0),
        name="fetch",
    )(after, *[in_hbm(array) for array, _ in parts])


def join_kernel(first, second, out):
    count = first.shape[0]
    for layer in range(out.shape[0]):
        out[layer, :count] = first[:, layer, :]
        out[layer, count:] = second[:, layer, :]


def join(first, second):
    count, layers, width = first.shape
    return pl.pallas_call(
        join_kernel,
        out_shape=jax.ShapeDtypeStruct((layers, 2 * count, width), first.dtype),
        in_specs=[VMEM, VMEM],
        out_specs=VMEM,
        compiler_params=pltpu.CompilerParams(vmem_limit_bytes=1 << 20),
        name="join",
    )(first, second)


def transcode_kernel(steps, order, ready, limit, near, far, bias, encoder, decoder, *rest):
    fetched = dict(zip(ready, rest))
    keep_out, send_out, ring, feats, sems = rest[len(ready) :]
    layers, half, width = near.shape

    def stream(step):
        source = fetched[step] if step in fetched else decoder.at[pair_index(*order[step], layers)]
        return pltpu.make_async_copy(source, ring.at[step % SLOTS], sems.at[step % SLOTS])

    for i in range(min(2, SLOTS, len(order))):
        stream(i).start()

    block = half >> len(steps)
    place = lax.broadcasted_iota(jnp.int32, (half, 1), 0)
    slot = lax.div(place, block) if block & (block - 1) else place >> (block.bit_length() - 1)
    me = lax.axis_index("pair")

    def positions(owner):
        start = owner
        for bit, (even_mask, odd_mask) in enumerate(steps):
            mask = even_mask + (odd_mask - even_mask) * (start & 1)
            owner = owner ^ (((slot >> bit) & 1) * mask)
        return owner * block + place - slot * block

    keep = jnp.concatenate([positions(me), positions(me ^ 1)], axis=0) < limit[0]

    for layer in range(layers):
        x = jnp.concatenate([near[layer], far[layer]], axis=0)
        pre = jnp.dot(x, encoder[layer], preferred_element_type=F32) + bias[layer][None, :]
        feats[layer] = jnp.where(keep, jnp.maximum(pre, 0.0), 0.0).astype(BF16)
        if 2 <= layer + 1 < min(SLOTS, len(order)):
            stream(layer + 1).start()

    total = None
    for step, (source, target) in enumerate(order):
        stream(step).wait()
        term = jnp.dot(feats[source], ring[step % SLOTS], preferred_element_type=F32)
        total = term if source == 0 else total + term
        if step + SLOTS < len(order):
            stream(step + SLOTS).start()
        if source == target:
            keep_out[target] = total[:half]
            send_out[target] = total[half:]


def transcode(steps, order, ready, limit, near, far, bias, encoder, decoder, fetched):
    layers, half, width = near.shape
    features = decoder.shape[1]
    out = jax.ShapeDtypeStruct((layers, half, width), F32)
    need = SLOTS * features * width * 2 + layers * 2 * half * features * 2 + 16 * half * width
    return pl.pallas_call(
        functools.partial(transcode_kernel, steps, order, ready),
        out_shape=(out, out),
        in_specs=[SMEM, VMEM, VMEM, VMEM, VMEM, ANY] + [VMEM] * len(fetched),
        out_specs=(VMEM, VMEM),
        scratch_shapes=[
            pltpu.VMEM((SLOTS, features, width), BF16),
            pltpu.VMEM((layers, 2 * half, features), BF16),
            pltpu.SemaphoreType.DMA((SLOTS,)),
        ],
        compiler_params=pltpu.CompilerParams(vmem_limit_bytes=need + (5 << 20)),
        name="transcode",
    )(limit, near, far, bias, encoder, in_hbm(decoder), *fetched)


def body(size, layer_inputs, encoder, enc_bias, decoder, dec_bias, valid_count):
    layers, width, features = encoder.shape
    steps = exchange_steps(size)
    order = [(source, target) for target in range(layers) for source in range(target + 1)]
    ready = [len(order) // 2, len(order) // 2 + 2][: len(steps) - 1]
    fetched = []
    held = layer_inputs
    for i, masks in enumerate(steps):
        came = swap(held, masks, size)
        parts = [(held, None)] if i == 0 else []
        hidden = 2 * features * width
        if i < len(ready):
            parts.append((decoder, pair_index(*order[ready[i]], layers)))
        if i == len(steps) - 1:
            parts.append((enc_bias, None))
            hidden = 4 * layers * features * width
        came, *got = lax.optimization_barrier((came, *(fetch(held, parts, hidden) if parts else ())))
        held = join(got.pop(0), came) if i == 0 else jnp.concatenate([held, came], axis=1)
        if i == len(steps) - 1:
            enc_bias = got.pop()
        fetched += got
    far = swap(held, (1, 1), size)
    total, sent = transcode(steps, order, ready, valid_count, held, far, enc_bias, encoder, decoder, fetched)
    total = total + swap(sent, (1, 1), size)
    for i, masks in reversed(list(enumerate(steps))):
        count = total.shape[1] // 2
        total, sent = total[:, :count], total[:, count:]
        total = total + swap(sent if i == 0 else sent.astype(BF16), masks, size).astype(F32)
    return jnp.swapaxes(total, 0, 1) + dec_bias[None, :, :]


def solution(mesh):
    return jax.shard_map(
        functools.partial(body, mesh.shape["pair"]),
        mesh=mesh,
        in_specs=(
            P(("groups", "pair"), None, None),
            P(None, None, "pair"),
            P(None, "pair"),
            P(None, "pair", None),
            P(),
            P("groups"),
        ),
        out_specs=P(("groups", "pair"), None, None),
        check_vma=False,
    )
```

```python
import functools

import jax
import jax.numpy as jnp
from jax import lax
from jax.experimental import pallas as pl
from jax.experimental.pallas import tpu as pltpu
from jax.sharding import PartitionSpec as P

BF16, F32 = jnp.bfloat16, jnp.float32
VMEM = pl.BlockSpec(memory_space=pltpu.VMEM)
SMEM = pl.BlockSpec(memory_space=pltpu.SMEM)
ANY = pl.BlockSpec(memory_space=pl.ANY)
SLOTS = 4


def pair_index(source, target, layers):
    return source * layers - source * (source - 1) // 2 + (target - source)


def in_hbm(value):
    return pltpu.with_memory_space_constraint(value, pltpu.HBM)


def exchange_steps(size):
    masks = [1 << bit for bit in reversed(range(1, size.bit_length() - 1))]
    steps = [(mask, mask) for mask in masks]
    if len(steps) >= 2:
        steps[-2:] = [(masks[-2], masks[-1]), (masks[-1], masks[-2])]
    return steps


def swap(value, masks, size):
    return lax.ppermute(value, "pair", [(i, i ^ masks[i % 2]) for i in range(size)])


def fetch_kernel(indices, *refs):
    count = len(indices)
    sources, outs, sems = refs[1 : 1 + count], refs[1 + count : -1], refs[-1]
    copies = [
        pltpu.make_async_copy(source if index is None else source.at[index, pl.ds(0, out.shape[0])], out, sems.at[i])
        for i, (index, source, out) in enumerate(zip(indices, sources, outs))
    ]
    for copy in copies:
        copy.start()
    for copy in copies:
        copy.wait()


def fetch(after, parts, hidden):
    shapes = [
        jax.ShapeDtypeStruct(array.shape if index is None else (*rows, array.shape[2]), array.dtype)
        for array, index, *rows in parts
    ]
    return pl.pallas_call(
        functools.partial(fetch_kernel, [part[1] for part in parts]),
        out_shape=tuple(shapes),
        in_specs=[ANY] * (1 + len(parts)),
        out_specs=tuple(VMEM for _ in shapes),
        scratch_shapes=[pltpu.SemaphoreType.DMA((len(parts),))],
        compiler_params=pltpu.CompilerParams(vmem_limit_bytes=1 << 20),
        cost_estimate=pl.CostEstimate(flops=0, bytes_accessed=hidden, transcendentals=0),
        name="fetch",
    )(after, *[in_hbm(part[0]) for part in parts])


def join_kernel(first, second, out):
    count = first.shape[0]
    for layer in range(out.shape[0]):
        out[layer, :count] = first[:, layer, :]
        out[layer, count:] = second[:, layer, :]


def join(first, second):
    count, layers, width = first.shape
    return pl.pallas_call(
        join_kernel,
        out_shape=jax.ShapeDtypeStruct((layers, 2 * count, width), first.dtype),
        in_specs=[VMEM, VMEM],
        out_specs=VMEM,
        compiler_params=pltpu.CompilerParams(vmem_limit_bytes=1 << 20),
        name="join",
    )(first, second)


def transcode_kernel(steps, order, ready, limit, near, far, bias, encoder, decoder, *rest):
    fetched = dict(zip(ready, rest))
    keep_out, send_out, ring, feats, sems = rest[len(ready) :]
    layers, half, width = near.shape

    class Stream:
        def __init__(self, step):
            slot, ahead = step % SLOTS, fetched.get(step)
            rows = 0 if ahead is None else ahead.shape[0]
            matrix = decoder.at[pair_index(*order[step], layers)]
            self.copies = []
            if rows:
                self.copies.append(pltpu.make_async_copy(ahead, ring.at[slot, pl.ds(0, rows)], sems.at[1, slot]))
            if rows < ring.shape[1]:
                rest_rows = pl.ds(rows, ring.shape[1] - rows)
                self.copies.append(
                    pltpu.make_async_copy(matrix.at[rest_rows], ring.at[slot, rest_rows], sems.at[0, slot])
                )

        def start(self):
            for copy in self.copies:
                copy.start()

        def wait(self):
            for copy in self.copies:
                copy.wait()

    stream = Stream

    for i in range(min(2, SLOTS, len(order))):
        stream(i).start()

    block = half >> len(steps)
    place = lax.broadcasted_iota(jnp.int32, (half, 1), 0)
    slot = lax.div(place, block) if block & (block - 1) else place >> (block.bit_length() - 1)
    me = lax.axis_index("pair")

    def positions(owner):
        start = owner
        for bit, (even_mask, odd_mask) in enumerate(steps):
            mask = even_mask + (odd_mask - even_mask) * (start & 1)
            owner = owner ^ (((slot >> bit) & 1) * mask)
        return owner * block + place - slot * block

    keep = jnp.concatenate([positions(me), positions(me ^ 1)], axis=0) < limit[0]

    for layer in range(layers):
        x = jnp.concatenate([near[layer], far[layer]], axis=0)
        pre = jnp.dot(x, encoder[layer], preferred_element_type=F32) + bias[layer][None, :]
        feats[layer] = jnp.where(keep, jnp.maximum(pre, 0.0), 0.0).astype(BF16)
        if 2 <= layer + 1 < min(SLOTS, len(order)):
            stream(layer + 1).start()

    total = None
    for step, (source, target) in enumerate(order):
        stream(step).wait()
        term = jnp.dot(feats[source], ring[step % SLOTS], preferred_element_type=F32)
        total = term if source == 0 else total + term
        if step + SLOTS < len(order):
            stream(step + SLOTS).start()
        if source == target:
            keep_out[target] = total[:half]
            send_out[target] = total[half:]


def transcode(steps, order, ready, limit, near, far, bias, encoder, decoder, fetched):
    layers, half, width = near.shape
    features = decoder.shape[1]
    out = jax.ShapeDtypeStruct((layers, half, width), F32)
    need = SLOTS * features * width * 2 + layers * 2 * half * features * 2 + 16 * half * width
    return pl.pallas_call(
        functools.partial(transcode_kernel, steps, order, ready),
        out_shape=(out, out),
        in_specs=[SMEM, VMEM, VMEM, VMEM, VMEM, ANY] + [VMEM] * len(fetched),
        out_specs=(VMEM, VMEM),
        scratch_shapes=[
            pltpu.VMEM((SLOTS, features, width), BF16),
            pltpu.VMEM((layers, 2 * half, features), BF16),
            pltpu.SemaphoreType.DMA((2, SLOTS)),
        ],
        compiler_params=pltpu.CompilerParams(vmem_limit_bytes=need + (5 << 20)),
        name="transcode",
    )(limit, near, far, bias, encoder, in_hbm(decoder), *fetched)


def body(size, layer_inputs, encoder, enc_bias, decoder, dec_bias, valid_count):
    layers, width, features = encoder.shape
    steps = exchange_steps(size)
    order = [(source, target) for target in range(layers) for source in range(target + 1)]
    early = [(len(order) // 2, features), (len(order) // 2 + 2, features * 5 // 8)]
    fetched = []
    held = layer_inputs
    for i, masks in enumerate(steps):
        came = swap(held, masks, size)
        parts = [(held, None)] if i == 0 else []
        hidden = 2 * features * width
        if i < len(early):
            step, rows = early[i]
            parts.append((decoder, pair_index(*order[step], layers), rows))
        if i == len(steps) - 1:
            parts.append((enc_bias, None))
            hidden = 4 * layers * features * width
        came, *got = lax.optimization_barrier((came, *(fetch(held, parts, hidden) if parts else ())))
        held = join(got.pop(0), came) if i == 0 else jnp.concatenate([held, came], axis=1)
        if i == len(steps) - 1:
            enc_bias = got.pop()
        fetched += got
    far = swap(held, (1, 1), size)
    total, sent = transcode(steps, order, [step for step, _ in early], valid_count, held, far, enc_bias, encoder, decoder, fetched)
    total = total + swap(sent, (1, 1), size)
    for i, masks in reversed(list(enumerate(steps))):
        count = total.shape[1] // 2
        total, sent = total[:, :count], total[:, count:]
        total = total + swap(sent if i == 0 else sent.astype(BF16), masks, size).astype(F32)
    return jnp.swapaxes(total, 0, 1) + dec_bias[None, :, :]


def solution(mesh):
    return jax.shard_map(
        functools.partial(body, mesh.shape["pair"]),
        mesh=mesh,
        in_specs=(
            P(("groups", "pair"), None, None),
            P(None, None, "pair"),
            P(None, "pair"),
            P(None, "pair", None),
            P(),
            P("groups"),
        ),
        out_specs=P(("groups", "pair"), None, None),
        check_vma=False,
    )
```

```python
import functools

import jax
import jax.numpy as jnp
from jax import lax
from jax.experimental import pallas as pl
from jax.experimental.pallas import tpu as pltpu
from jax.sharding import PartitionSpec as P

BF16, F32 = jnp.bfloat16, jnp.float32
VMEM = pl.BlockSpec(memory_space=pltpu.VMEM)
SMEM = pl.BlockSpec(memory_space=pltpu.SMEM)
ANY = pl.BlockSpec(memory_space=pl.ANY)
SLOTS = 4
CHUNK = 768


def pair_index(source, target, layers):
    return source * layers - source * (source - 1) // 2 + (target - source)


def in_hbm(value):
    return pltpu.with_memory_space_constraint(value, pltpu.HBM)


def exchange_steps(size):
    masks = [1 << bit for bit in reversed(range(1, size.bit_length() - 1))]
    steps = [(mask, mask) for mask in masks]
    if len(steps) >= 2:
        steps[-2:] = [(masks[-2], masks[-1]), (masks[-1], masks[-2])]
    return steps


def swap(value, masks, size):
    return lax.ppermute(value, "pair", [(i, i ^ masks[i % 2]) for i in range(size)])


def fetch_kernel(indices, *refs):
    count = len(indices)
    sources, outs, sems = refs[1 : 1 + count], refs[1 + count : -1], refs[-1]
    copies = [
        pltpu.make_async_copy(source if index is None else source.at[index, pl.ds(0, out.shape[0])], out, sems.at[i])
        for i, (index, source, out) in enumerate(zip(indices, sources, outs))
    ]
    for copy in copies:
        copy.start()
    for copy in copies:
        copy.wait()


def fetch(after, parts, hidden):
    shapes = [
        jax.ShapeDtypeStruct(array.shape if index is None else (*rows, array.shape[2]), array.dtype)
        for array, index, *rows in parts
    ]
    return pl.pallas_call(
        functools.partial(fetch_kernel, [part[1] for part in parts]),
        out_shape=tuple(shapes),
        in_specs=[ANY] * (1 + len(parts)),
        out_specs=tuple(VMEM for _ in shapes),
        scratch_shapes=[pltpu.SemaphoreType.DMA((len(parts),))],
        compiler_params=pltpu.CompilerParams(vmem_limit_bytes=1 << 20),
        cost_estimate=pl.CostEstimate(flops=0, bytes_accessed=hidden, transcendentals=0),
        name="fetch",
    )(after, *[in_hbm(part[0]) for part in parts])


def join_kernel(first, second, out):
    count = first.shape[0]
    for layer in range(out.shape[0]):
        out[layer, :count] = first[:, layer, :]
        out[layer, count:] = second[:, layer, :]


def join(first, second):
    count, layers, width = first.shape
    return pl.pallas_call(
        join_kernel,
        out_shape=jax.ShapeDtypeStruct((layers, 2 * count, width), first.dtype),
        in_specs=[VMEM, VMEM],
        out_specs=VMEM,
        compiler_params=pltpu.CompilerParams(vmem_limit_bytes=1 << 20),
        name="join",
    )(first, second)


def chunks(width):
    return [(start, min(CHUNK, width - start)) for start in range(0, width, CHUNK)]


def transcode_kernel(steps, order, ready, limit, near, far, bias, encoder, decoder, *rest):
    fetched = dict(zip(ready, rest))
    keep_out, send_out, ring, feats, sems = rest[len(ready) :]
    layers, half, width = near.shape
    features = feats.shape[2]

    class Stream:
        def __init__(self, step):
            slot, ahead = step % SLOTS, fetched.get(step)
            rows = 0 if ahead is None else ahead.shape[0]
            matrix = decoder.at[pair_index(*order[step], layers)]
            self.copies = []
            if rows:
                self.copies.append(pltpu.make_async_copy(ahead, ring.at[slot, pl.ds(0, rows)], sems.at[1, slot]))
            if rows < ring.shape[1]:
                rest_rows = pl.ds(rows, ring.shape[1] - rows)
                self.copies.append(
                    pltpu.make_async_copy(matrix.at[rest_rows], ring.at[slot, rest_rows], sems.at[0, slot])
                )

        def start(self):
            for copy in self.copies:
                copy.start()

        def wait(self):
            for copy in self.copies:
                copy.wait()

    stream = Stream

    for i in range(min(2, SLOTS, len(order))):
        stream(i).start()

    block = half >> len(steps)
    place = lax.broadcasted_iota(jnp.int32, (half, 1), 0)
    slot = lax.div(place, block) if block & (block - 1) else place >> (block.bit_length() - 1)
    me = lax.axis_index("pair")

    def positions(owner):
        start = owner
        for bit, (even_mask, odd_mask) in enumerate(steps):
            mask = even_mask + (odd_mask - even_mask) * (start & 1)
            owner = owner ^ (((slot >> bit) & 1) * mask)
        return owner * block + place - slot * block

    keep = jnp.concatenate([positions(me), positions(me ^ 1)], axis=0) < limit[0]

    for layer in range(layers):
        x = jnp.concatenate([near[layer], far[layer]], axis=0)
        for start, count in chunks(features):
            columns = pl.ds(start, count)
            pre = jnp.dot(x, encoder[layer, :, columns], preferred_element_type=F32) + bias[pl.ds(layer, 1), columns]
            feats[layer, :, columns] = jnp.where(keep, jnp.maximum(pre, 0.0), 0.0).astype(BF16)
        if 2 <= layer + 1 < min(SLOTS, len(order)):
            stream(layer + 1).start()

    total = None
    for step, (source, target) in enumerate(order):
        stream(step).wait()
        terms = [
            jnp.dot(feats[source], ring[step % SLOTS, :, pl.ds(start, count)], preferred_element_type=F32)
            for start, count in chunks(width)
        ]
        term = jnp.concatenate(terms, axis=1)
        total = term if source == 0 else total + term
        if step + SLOTS < len(order):
            stream(step + SLOTS).start()
        if source == target:
            keep_out[target] = total[:half]
            send_out[target] = total[half:]


def transcode(steps, order, ready, limit, near, far, bias, encoder, decoder, fetched):
    layers, half, width = near.shape
    features = decoder.shape[1]
    out = jax.ShapeDtypeStruct((layers, half, width), F32)
    need = SLOTS * features * width * 2 + layers * 2 * half * features * 2 + 16 * half * width
    return pl.pallas_call(
        functools.partial(transcode_kernel, steps, order, ready),
        out_shape=(out, out),
        in_specs=[SMEM, VMEM, VMEM, VMEM, VMEM, ANY] + [VMEM] * len(fetched),
        out_specs=(VMEM, VMEM),
        scratch_shapes=[
            pltpu.VMEM((SLOTS, features, width), BF16),
            pltpu.VMEM((layers, 2 * half, features), BF16),
            pltpu.SemaphoreType.DMA((2, SLOTS)),
        ],
        compiler_params=pltpu.CompilerParams(vmem_limit_bytes=need + (3 << 20)),
        name="transcode",
    )(limit, near, far, bias, encoder, in_hbm(decoder), *fetched)


def body(size, layer_inputs, encoder, enc_bias, decoder, dec_bias, valid_count):
    layers, width, features = encoder.shape
    steps = exchange_steps(size)
    order = [(source, target) for target in range(layers) for source in range(target + 1)]
    early = [(len(order) // 2, features), (len(order) // 2 + 2, features * 5 // 8)]
    fetched = []
    held = layer_inputs
    for i, masks in enumerate(steps):
        came = swap(held, masks, size)
        parts = [(held, None)] if i == 0 else []
        hidden = 2 * features * width
        if i < len(early):
            step, rows = early[i]
            parts.append((decoder, pair_index(*order[step], layers), rows))
        if i == len(steps) - 1:
            parts.append((enc_bias, None))
            hidden = 4 * layers * features * width
        came, *got = lax.optimization_barrier((came, *(fetch(held, parts, hidden) if parts else ())))
        held = join(got.pop(0), came) if i == 0 else jnp.concatenate([held, came], axis=1)
        if i == len(steps) - 1:
            enc_bias = got.pop()
        fetched += got
    far = swap(held, (1, 1), size)
    total, sent = transcode(steps, order, [step for step, _ in early], valid_count, held, far, enc_bias, encoder, decoder, fetched)
    total = total + swap(sent, (1, 1), size)
    for i, masks in reversed(list(enumerate(steps))):
        count = total.shape[1] // 2
        total, sent = total[:, :count], total[:, count:]
        total = total + swap(sent if i == 0 else sent.astype(BF16), masks, size).astype(F32)
    return jnp.swapaxes(total, 0, 1) + dec_bias[None, :, :]


def solution(mesh):
    return jax.shard_map(
        functools.partial(body, mesh.shape["pair"]),
        mesh=mesh,
        in_specs=(
            P(("groups", "pair"), None, None),
            P(None, None, "pair"),
            P(None, "pair"),
            P(None, "pair", None),
            P(),
            P("groups"),
        ),
        out_specs=P(("groups", "pair"), None, None),
        check_vma=False,
    )
```

```python
import functools

import jax
import jax.numpy as jnp
from jax import lax
from jax.experimental import pallas as pl
from jax.experimental.pallas import tpu as pltpu
from jax.sharding import PartitionSpec as P

BF16, F32 = jnp.bfloat16, jnp.float32
VMEM = pl.BlockSpec(memory_space=pltpu.VMEM)
SMEM = pl.BlockSpec(memory_space=pltpu.SMEM)
ANY = pl.BlockSpec(memory_space=pl.ANY)
SLOTS = 4
CHUNK = 768


def pair_index(source, target, layers):
    return source * layers - source * (source - 1) // 2 + (target - source)


def in_hbm(value):
    return pltpu.with_memory_space_constraint(value, pltpu.HBM)


def exchange_steps(size):
    masks = [1 << bit for bit in reversed(range(1, size.bit_length() - 1))]
    steps = [(mask, mask) for mask in masks]
    if len(steps) >= 2:
        steps[-2:] = [(masks[-2], masks[-1]), (masks[-1], masks[-2])]
    return steps


def swap(value, masks, size):
    return lax.ppermute(value, "pair", [(i, i ^ masks[i % 2]) for i in range(size)])


def fetch_kernel(indices, *refs):
    count = len(indices)
    sources, outs, sems = refs[1 : 1 + count], refs[1 + count : -1], refs[-1]
    copies = [
        pltpu.make_async_copy(source if index is None else source.at[index, pl.ds(0, out.shape[0])], out, sems.at[i])
        for i, (index, source, out) in enumerate(zip(indices, sources, outs))
    ]
    for copy in copies:
        copy.start()
    for copy in copies:
        copy.wait()


def fetch(after, parts, hidden):
    shapes = [
        jax.ShapeDtypeStruct(array.shape if index is None else (*rows, array.shape[2]), array.dtype)
        for array, index, *rows in parts
    ]
    return pl.pallas_call(
        functools.partial(fetch_kernel, [part[1] for part in parts]),
        out_shape=tuple(shapes),
        in_specs=[ANY] * (1 + len(parts)),
        out_specs=tuple(VMEM for _ in shapes),
        scratch_shapes=[pltpu.SemaphoreType.DMA((len(parts),))],
        compiler_params=pltpu.CompilerParams(vmem_limit_bytes=1 << 20),
        cost_estimate=pl.CostEstimate(flops=0, bytes_accessed=hidden, transcendentals=0),
        name="fetch",
    )(after, *[in_hbm(part[0]) for part in parts])


def join_kernel(first, second, out):
    count = first.shape[0]
    for layer in range(out.shape[0]):
        out[layer, :count] = first[:, layer, :]
        out[layer, count:] = second[:, layer, :]


def join(first, second):
    count, layers, width = first.shape
    return pl.pallas_call(
        join_kernel,
        out_shape=jax.ShapeDtypeStruct((layers, 2 * count, width), first.dtype),
        in_specs=[VMEM, VMEM],
        out_specs=VMEM,
        compiler_params=pltpu.CompilerParams(vmem_limit_bytes=1 << 20),
        name="join",
    )(first, second)


def chunks(width):
    return [(start, min(CHUNK, width - start)) for start in range(0, width, CHUNK)]


def transcode_kernel(steps, order, ready, limit, near, far, bias, encoder, decoder, *rest):
    fetched = dict(zip(ready, rest))
    keep_out, send_out, ring, feats, sems = rest[len(ready) :]
    layers, half, width = near.shape
    features = feats.shape[2]

    class Stream:
        def __init__(self, step):
            slot, ahead = step % SLOTS, fetched.get(step)
            rows = 0 if ahead is None else ahead.shape[0]
            matrix = decoder.at[pair_index(*order[step], layers)]
            self.copies = []
            if rows:
                self.copies.append(pltpu.make_async_copy(ahead, ring.at[slot, pl.ds(0, rows)], sems.at[1, slot]))
            if rows < ring.shape[1]:
                rest_rows = pl.ds(rows, ring.shape[1] - rows)
                self.copies.append(
                    pltpu.make_async_copy(matrix.at[rest_rows], ring.at[slot, rest_rows], sems.at[0, slot])
                )

        def start(self):
            for copy in self.copies:
                copy.start()

        def wait(self):
            for copy in self.copies:
                copy.wait()

    stream = Stream

    for i in range(min(2, SLOTS, len(order))):
        stream(i).start()

    block = half >> len(steps)
    place = lax.broadcasted_iota(jnp.int32, (half, 1), 0)
    slot = lax.div(place, block) if block & (block - 1) else place >> (block.bit_length() - 1)
    me = lax.axis_index("pair")

    def positions(owner):
        start = owner
        for bit, (even_mask, odd_mask) in enumerate(steps):
            mask = even_mask + (odd_mask - even_mask) * (start & 1)
            owner = owner ^ (((slot >> bit) & 1) * mask)
        return owner * block + place - slot * block

    keep = jnp.concatenate([positions(me), positions(me ^ 1)], axis=0) < limit[0]

    for layer in range(layers):
        x = jnp.concatenate([near[layer], far[layer]], axis=0)
        for start, count in chunks(features):
            columns = pl.ds(start, count)
            pre = jnp.dot(x, encoder[layer, :, columns], preferred_element_type=F32) + bias[pl.ds(layer, 1), columns]
            feats[layer, :, columns] = jnp.where(keep, jnp.maximum(pre, 0.0), 0.0).astype(BF16)
        if 2 <= layer + 1 < min(SLOTS, len(order)):
            stream(layer + 1).start()

    total = None
    for step, (source, target) in enumerate(order):
        stream(step).wait()
        terms = [
            jnp.dot(feats[source], ring[step % SLOTS, :, pl.ds(start, count)], preferred_element_type=F32)
            for start, count in chunks(width)
        ]
        term = jnp.concatenate(terms, axis=1)
        total = term if source == 0 else total + term
        if step + SLOTS < len(order):
            stream(step + SLOTS).start()
        if source == target:
            keep_out[target] = total[:half]
            send_out[target] = total[half:]


def transcode(steps, order, ready, limit, near, far, bias, encoder, decoder, fetched):
    layers, half, width = near.shape
    features = decoder.shape[1]
    out = jax.ShapeDtypeStruct((layers, half, width), F32)
    need = SLOTS * features * width * 2 + layers * 2 * half * features * 2 + 16 * half * width
    return pl.pallas_call(
        functools.partial(transcode_kernel, steps, order, ready),
        out_shape=(out, out),
        in_specs=[SMEM, VMEM, VMEM, VMEM, VMEM, ANY] + [VMEM] * len(fetched),
        out_specs=(VMEM, VMEM),
        scratch_shapes=[
            pltpu.VMEM((SLOTS, features, width), BF16),
            pltpu.VMEM((layers, 2 * half, features), BF16),
            pltpu.SemaphoreType.DMA((2, SLOTS)),
        ],
        compiler_params=pltpu.CompilerParams(vmem_limit_bytes=need + (3 << 20)),
        name="transcode",
    )(limit, near, far, bias, encoder, in_hbm(decoder), *fetched)


def body(size, layer_inputs, encoder, enc_bias, decoder, dec_bias, valid_count):
    layers, width, features = encoder.shape
    steps = exchange_steps(size)
    order = [(source, target) for target in range(layers) for source in range(target + 1)]
    early = [(len(order) // 2, features), (len(order) // 2 + 2, features * 5 // 8)]
    fetched = []
    held = layer_inputs
    for i, masks in enumerate(steps):
        came = swap(held, masks, size)
        first = swap(held, (1, 1), size) if i == len(steps) - 1 else None
        parts = [(held, None)] if i == 0 else []
        hidden = 2 * features * width
        if i < len(early):
            step, rows = early[i]
            parts.append((decoder, pair_index(*order[step], layers), rows))
        if i == len(steps) - 1:
            parts.append((enc_bias, None))
            hidden = 4 * layers * features * width
        came, *got = lax.optimization_barrier((came, *(fetch(held, parts, hidden) if parts else ())))
        held = join(got.pop(0), came) if i == 0 else jnp.concatenate([held, came], axis=1)
        if i == len(steps) - 1:
            enc_bias = got.pop()
        fetched += got
    far = jnp.concatenate([first, swap(came, (1, 1), size)], axis=1)
    total, sent = transcode(steps, order, [step for step, _ in early], valid_count, held, far, enc_bias, encoder, decoder, fetched)
    total = total + swap(sent, (1, 1), size)
    for i, masks in reversed(list(enumerate(steps))):
        count = total.shape[1] // 2
        total, sent = total[:, :count], total[:, count:]
        total = total + swap(sent if i == 0 else sent.astype(BF16), masks, size).astype(F32)
    return jnp.swapaxes(total, 0, 1) + dec_bias[None, :, :]


def solution(mesh):
    return jax.shard_map(
        functools.partial(body, mesh.shape["pair"]),
        mesh=mesh,
        in_specs=(
            P(("groups", "pair"), None, None),
            P(None, None, "pair"),
            P(None, "pair"),
            P(None, "pair", None),
            P(),
            P("groups"),
        ),
        out_specs=P(("groups", "pair"), None, None),
        check_vma=False,
    )
```

```python
import functools

import jax
import jax.numpy as jnp
from jax import lax
from jax.experimental import pallas as pl
from jax.experimental.pallas import tpu as pltpu
from jax.sharding import PartitionSpec as P

BF16, F32 = jnp.bfloat16, jnp.float32
VMEM = pl.BlockSpec(memory_space=pltpu.VMEM)
SMEM = pl.BlockSpec(memory_space=pltpu.SMEM)
ANY = pl.BlockSpec(memory_space=pl.ANY)
SLOTS = 4
CHUNK = 512


def pair_index(source, target, layers):
    return source * layers - source * (source - 1) // 2 + (target - source)


def in_hbm(value):
    return pltpu.with_memory_space_constraint(value, pltpu.HBM)


def exchange_steps(size):
    masks = [1 << bit for bit in reversed(range(1, size.bit_length() - 1))]
    steps = [(mask, mask) for mask in masks]
    if len(steps) >= 2:
        steps[-2:] = [(masks[-2], masks[-1]), (masks[-1], masks[-2])]
    return steps


def swap(value, masks, size):
    return lax.ppermute(value, "pair", [(i, i ^ masks[i % 2]) for i in range(size)])


def fetch_kernel(indices, *refs):
    count = len(indices)
    sources, outs, sems = refs[1 : 1 + count], refs[1 + count : -1], refs[-1]
    copies = [
        pltpu.make_async_copy(source if index is None else source.at[index, pl.ds(0, out.shape[0])], out, sems.at[i])
        for i, (index, source, out) in enumerate(zip(indices, sources, outs))
    ]
    for copy in copies:
        copy.start()
    for copy in copies:
        copy.wait()


def fetch(after, parts, hidden):
    shapes = [
        jax.ShapeDtypeStruct(array.shape if index is None else (*rows, array.shape[2]), array.dtype)
        for array, index, *rows in parts
    ]
    return pl.pallas_call(
        functools.partial(fetch_kernel, [part[1] for part in parts]),
        out_shape=tuple(shapes),
        in_specs=[ANY] * (1 + len(parts)),
        out_specs=tuple(VMEM for _ in shapes),
        scratch_shapes=[pltpu.SemaphoreType.DMA((len(parts),))],
        compiler_params=pltpu.CompilerParams(vmem_limit_bytes=1 << 20),
        cost_estimate=pl.CostEstimate(flops=0, bytes_accessed=hidden, transcendentals=0),
        name="fetch",
    )(after, *[in_hbm(part[0]) for part in parts])


def join_kernel(first, second, out):
    count = first.shape[0]
    for layer in range(out.shape[0]):
        out[layer, :count] = first[:, layer, :]
        out[layer, count:] = second[:, layer, :]


def join(first, second):
    count, layers, width = first.shape
    return pl.pallas_call(
        join_kernel,
        out_shape=jax.ShapeDtypeStruct((layers, 2 * count, width), first.dtype),
        in_specs=[VMEM, VMEM],
        out_specs=VMEM,
        compiler_params=pltpu.CompilerParams(vmem_limit_bytes=1 << 20),
        name="join",
    )(first, second)


def chunks(width):
    return [(start, min(CHUNK, width - start)) for start in range(0, width, CHUNK)]


def transcode_kernel(steps, order, ready, limit, near, far, bias, encoder, decoder, *rest):
    fetched = dict(zip(ready, rest))
    keep_out, send_out, ring, feats, sems = rest[len(ready) :]
    layers, half, width = near.shape
    features = feats.shape[2]

    class Stream:
        def __init__(self, step):
            slot, ahead = step % SLOTS, fetched.get(step)
            rows = 0 if ahead is None else ahead.shape[0]
            matrix = decoder.at[pair_index(*order[step], layers)]
            self.copies = []
            if rows:
                self.copies.append(pltpu.make_async_copy(ahead, ring.at[slot, pl.ds(0, rows)], sems.at[1, slot]))
            if rows < ring.shape[1]:
                rest_rows = pl.ds(rows, ring.shape[1] - rows)
                self.copies.append(
                    pltpu.make_async_copy(matrix.at[rest_rows], ring.at[slot, rest_rows], sems.at[0, slot])
                )

        def start(self):
            for copy in self.copies:
                copy.start()

        def wait(self):
            for copy in self.copies:
                copy.wait()

    stream = Stream

    for i in range(min(2, SLOTS, len(order))):
        stream(i).start()

    block = half >> len(steps)
    place = lax.broadcasted_iota(jnp.int32, (half, 1), 0)
    slot = lax.div(place, block) if block & (block - 1) else place >> (block.bit_length() - 1)
    me = lax.axis_index("pair")

    def positions(owner):
        start = owner
        for bit, (even_mask, odd_mask) in enumerate(steps):
            mask = even_mask + (odd_mask - even_mask) * (start & 1)
            owner = owner ^ (((slot >> bit) & 1) * mask)
        return owner * block + place - slot * block

    keep = jnp.concatenate([positions(me), positions(me ^ 1)], axis=0) < limit[0]

    for layer in range(layers):
        x = jnp.concatenate([near[layer], far[layer]], axis=0)
        for start, count in chunks(features):
            columns = pl.ds(start, count)
            pre = jnp.dot(x, encoder[layer, :, columns], preferred_element_type=F32) + bias[pl.ds(layer, 1), columns]
            feats[layer, :, columns] = jnp.where(keep, jnp.maximum(pre, 0.0), 0.0).astype(BF16)
        if 2 <= layer + 1 < min(SLOTS, len(order)):
            stream(layer + 1).start()

    total = None
    for step, (source, target) in enumerate(order):
        stream(step).wait()
        terms = [
            jnp.dot(feats[source], ring[step % SLOTS, :, pl.ds(start, count)], preferred_element_type=F32)
            for start, count in chunks(width)
        ]
        term = jnp.concatenate(terms, axis=1)
        total = term if source == 0 else total + term
        if step + SLOTS < len(order):
            stream(step + SLOTS).start()
        if source == target:
            keep_out[target] = total[:half]
            send_out[target] = total[half:]


def transcode(steps, order, ready, limit, near, far, bias, encoder, decoder, fetched):
    layers, half, width = near.shape
    features = decoder.shape[1]
    out = jax.ShapeDtypeStruct((layers, half, width), F32)
    need = SLOTS * features * width * 2 + layers * 2 * half * features * 2 + 16 * half * width
    return pl.pallas_call(
        functools.partial(transcode_kernel, steps, order, ready),
        out_shape=(out, out),
        in_specs=[SMEM, VMEM, VMEM, VMEM, VMEM, ANY] + [VMEM] * len(fetched),
        out_specs=(VMEM, VMEM),
        scratch_shapes=[
            pltpu.VMEM((SLOTS, features, width), BF16),
            pltpu.VMEM((layers, 2 * half, features), BF16),
            pltpu.SemaphoreType.DMA((2, SLOTS)),
        ],
        compiler_params=pltpu.CompilerParams(vmem_limit_bytes=need + (3 << 20)),
        name="transcode",
    )(limit, near, far, bias, encoder, in_hbm(decoder), *fetched)


def body(size, layer_inputs, encoder, enc_bias, decoder, dec_bias, valid_count):
    layers, width, features = encoder.shape
    steps = exchange_steps(size)
    order = [(source, target) for target in range(layers) for source in range(target + 1)]
    early = [(len(order) // 2, features), (len(order) // 2 + 2, features * 5 // 8)]
    fetched = []
    held = layer_inputs
    for i, masks in enumerate(steps):
        came = swap(held, masks, size)
        first = swap(held, (1, 1), size) if i == len(steps) - 1 else None
        parts = [(held, None)] if i == 0 else []
        hidden = 2 * features * width
        if i < len(early):
            step, rows = early[i]
            parts.append((decoder, pair_index(*order[step], layers), rows))
        if i == len(steps) - 1:
            parts.append((enc_bias, None))
            hidden = 4 * layers * features * width
        came, *got = lax.optimization_barrier((came, *(fetch(held, parts, hidden) if parts else ())))
        held = join(got.pop(0), came) if i == 0 else jnp.concatenate([held, came], axis=1)
        if i == len(steps) - 1:
            enc_bias = got.pop()
        fetched += got
    far = jnp.concatenate([first, swap(came, (1, 1), size)], axis=1)
    total, sent = transcode(steps, order, [step for step, _ in early], valid_count, held, far, enc_bias, encoder, decoder, fetched)
    total = total + swap(sent, (1, 1), size)
    for i, masks in reversed(list(enumerate(steps))):
        count = total.shape[1] // 2
        total, sent = total[:, :count], total[:, count:]
        total = total + swap(sent if i == 0 else sent.astype(BF16), masks, size).astype(F32)
    return jnp.swapaxes(total, 0, 1) + dec_bias[None, :, :]


def solution(mesh):
    return jax.shard_map(
        functools.partial(body, mesh.shape["pair"]),
        mesh=mesh,
        in_specs=(
            P(("groups", "pair"), None, None),
            P(None, None, "pair"),
            P(None, "pair"),
            P(None, "pair", None),
            P(),
            P("groups"),
        ),
        out_specs=P(("groups", "pair"), None, None),
        check_vma=False,
    )
```
